512 devices in a mesh: gx: 128 (over y_hi, z, x), trait: 4 (over y_lo, core).
Axes of the slice: x: 4, y: 4 (y_hi: 2, y_lo: 2; y = y_hi * 2 + y_lo), z: 16, core: 2. Of those that a mesh axis runs over, the one named last changes fastest.
Arguments:
- initial: float32 [1024, 128, 1024], P('gx', None, 'trait'), may hold values from 0.2 to 2
- section_one: float32 [1024, 128, 1024], P('gx', None, 'trait'), may hold values from 0.2 to 2
- section_two: float32 [1024, 128, 1024], P('gx', None, 'trait'), may hold values from 0.2 to 2
- kernels: bfloat16 [2, 1024, 1024], P(None, None, 'trait'), may hold values from -0.1875 to 0.1875
- growth: float32 [1024], P('trait'), may hold values from -3 to 3
- death_rate: float32 [1024], P('trait'), may hold values from 0.5 to 8
Outputs:
- new_one: float32 [1024, 128, 1024], P('gx', None, 'trait')
- new_two: float32 [1024, 128, 1024], P('gx', None, 'trait')
The draws below stay inside these ranges and needn't reach their ends.
All inputs are finite; a program needn't handle non-finite values.
Results may differ from the reference program's by a relative error of at most 0.002.
Values may be sent and summed in bfloat16 or wider, within the bound.
A program may use at most 64 MiB of HBM per device.

```python
import math
import jax
import jax.numpy as jnp
from jax import lax

M = 1024
NY = 128
NX = 1024


def block_levels(rng, shape, split, low, top_value):
    loudness = 1.0
    for dim, parts in split:
        heights = jax.random.uniform(jax.random.fold_in(jax.random.fold_in(rng, 6), dim), (parts,), jnp.float32, low / len(split), top_value / len(split))
        loudness = loudness * jnp.repeat(jnp.exp(heights), shape[dim] // parts).reshape((-1,) + (1,) * (len(shape) - 1 - dim))
    return loudness


def normal_values(own_key, shape, scale, reach, pieces=(), dtype=jnp.bfloat16):
    array = scale * jax.random.normal(own_key, shape, jnp.float32)
    if pieces:
        array = array * block_levels(own_key, shape, pieces, -0.22, 0.18)
    return jnp.clip(array, -reach, reach).astype(dtype)


def setup_inputs(seed: int = 0) -> dict:
    splits = jax.random.split(jax.random.key(seed), 7)
    return {
        "initial": jnp.clip(jnp.exp(math.log(2.0) - 2.3025851 * jax.random.uniform(splits[0], (NX, NY, M), jnp.float32) ** block_levels(splits[0], (NX, NY, M), ((0, 128), (2, 4)), -0.2, 0.2)), 0.2, 2.0),
        "section_one": jnp.clip(jnp.exp(math.log(2.0) - 2.3025851 * jax.random.uniform(splits[1], (NX, NY, M), jnp.float32) ** block_levels(splits[1], (NX, NY, M), ((0, 128), (2, 4)), -0.2, 0.2)), 0.2, 2.0),
        "section_two": jnp.clip(jnp.exp(math.log(2.0) - 2.3025851 * jax.random.uniform(splits[2], (NX, NY, M), jnp.float32) ** block_levels(splits[2], (NX, NY, M), ((0, 128), (2, 4)), -0.2, 0.2)), 0.2, 2.0),
        "kernels": normal_values(splits[3], (2, M, M), M ** -0.5, 0.1875, ((2, 4),)),
        "growth": normal_values(splits[4], (M,), 1.0, 3.0, ((0, 4),), jnp.float32),
        "death_rate": jnp.clip(jnp.exp(math.log(8.0) - 2.7725887 * jax.random.uniform(splits[5], (M,), jnp.float32) ** block_levels(splits[5], (M,), ((0, 4),), -0.2, 0.2)), 0.5, 8.0),
    }


DIFFUSION = 0.25
STEP_SIZE = 0.5


def rounded(field):
    return lax.optimization_barrier(field.astype(jnp.bfloat16)).astype(jnp.float32)


def explicit(field, kernels, growth):
    lapl = (jnp.roll(field, 1, 0) + jnp.roll(field, -1, 0) + jnp.roll(field, 1, 1)
            + jnp.roll(field, -1, 1) - 4.0 * field)
    flat = rounded(field).reshape(-1, M)
    kern = kernels.astype(jnp.float32)
    compete = rounded(jnp.dot(flat, kern[0], preferred_element_type=jnp.float32)).reshape(field.shape)
    mutate = rounded(jnp.dot(flat, kern[1], preferred_element_type=jnp.float32)).reshape(field.shape)
    return DIFFUSION * lapl + field * (growth - compete) + mutate - field


def reference(initial, section_one, section_two, kernels, growth, death_rate):
    first_dt = STEP_SIZE / 3.0
    second_dt = 2.0 * STEP_SIZE / 3.0
    expl_one = explicit(section_one, kernels, growth)
    expl_two = explicit(section_two, kernels, growth)
    full_one = expl_one - death_rate * section_one
    full_two = expl_two - death_rate * section_two
    new_one = (initial + first_dt * death_rate * section_one
               + STEP_SIZE * (5.0 / 12.0 * full_one - 1.0 / 12.0 * full_two)) / (1.0 + first_dt * death_rate)
    expl_new = explicit(new_one, kernels, growth)
    new_two = (new_one + second_dt * (expl_new - expl_one) + second_dt * death_rate * section_two
               + STEP_SIZE / 3.0 * (full_one + full_two)) / (1.0 + second_dt * death_rate)
    return new_one, new_two
```

```python
import functools

import jax
import jax.numpy as jnp
from jax import lax
from jax.experimental import pallas as pl
from jax.experimental.pallas import tpu as pltpu
from jax.sharding import PartitionSpec as P

MESH = pl.DeviceIdType.MESH
DIFFUSION = 0.25
STEP_SIZE = 0.5
FIRST_DT = STEP_SIZE / 3.0
SECOND_DT = 2.0 * STEP_SIZE / 3.0

GATHER_ORDER = (0, 7, 1, 2, 3, 4, 5, 6)
FIRST_PLAN = ((), (), (), (1,), (2,), (0, 3), (7, 4), (5,), (6,))
SEND_ORDER = (1, 2, 0, 3, 7, 4, 5, 6)
SECOND_PLAN = ((), (1,), (2,), (), (3,), (), (4, 0), (5, 7), (6,))


def kernel(
    ngx,
    initial, one, two, kernels, growth, death,
    out_one, out_two,
    s_one, s_two, s_init, weights, n_one, rest, sect, news, halo_s, halo_n,
    load_sem, init_sem, weight_sem, out_sem,
    cross_send, cross_recv, pair_send, pair_recv, relay_send, relay_recv, halo_send, halo_recv,
):
    planes, ny, owned = one.shape
    gx = lax.axis_index("gx")
    t = lax.axis_index("trait")
    half = ngx // 2
    pair = t + 1 - 2 * (t % 2)
    cross = (t + 2) % 4
    far = (pair + 2) % 4
    right = (gx + 1) % ngx
    left = (gx + ngx - 1) % ngx
    jump_r = (gx % half + 1) // half
    jump_l = (half - gx % half) // half
    t_r = (t + 2 * jump_r) % 4
    t_l = (t + 2 * jump_l) % 4

    loads = {}
    for p in GATHER_ORDER:
        loads[p] = (
            pltpu.make_async_copy(one.at[p], s_one.at[p], load_sem.at[0, p]),
            pltpu.make_async_copy(two.at[p], s_two.at[p], load_sem.at[1, p]),
        )
        loads[p][0].start()
        loads[p][1].start()
    load_w = pltpu.make_async_copy(kernels, weights, weight_sem)
    load_w.start()
    load_i = pltpu.make_async_copy(initial, s_init, init_sem)
    load_i.start()

    barrier = pltpu.get_barrier_semaphore()
    for device in ((gx, pair), (gx, cross), (right, t_r), (left, t_l)):
        pl.semaphore_signal(barrier, inc=1, device_id=device, device_id_type=MESH)
    pl.semaphore_wait(barrier, 4)

    def remote(src, dst, send, recv, device):
        return pltpu.make_async_remote_copy(
            src_ref=src, dst_ref=dst, send_sem=send, recv_sem=recv, device_id=device, device_id_type=MESH
        )

    started = []

    def start(copy):
        copy.start()
        started.append(copy)

    def spread(buf, s, p):
        mine = buf.at[p, t]
        start(remote(mine, mine, cross_send.at[s, p], cross_recv.at[s, p], (gx, cross)))
        start(remote(mine, mine, pair_send.at[s, p], pair_recv.at[s, p], (gx, pair)))

    def relay(buf, halo, s, p):
        theirs = buf.at[p, cross]
        remote(theirs, theirs, cross_send.at[s, p], cross_recv.at[s, p], (gx, cross)).wait_recv()
        start(remote(theirs, theirs, relay_send.at[s, p], relay_recv.at[s, p], (gx, pair)))
        if p == planes - 1:
            start(remote(buf.at[p, t_r], halo.at[0], halo_send.at[s, 0], halo_recv.at[s, 0], (right, t_r)))
        if p == 0:
            start(remote(buf.at[p, t_l], halo.at[1], halo_send.at[s, 1], halo_recv.at[s, 1], (left, t_l)))

    def gathered(buf, halo, s, p):
        remote(buf.at[p, pair], buf.at[p, pair], pair_send.at[s, p], pair_recv.at[s, p], (gx, pair)).wait_recv()
        remote(buf.at[p, far], buf.at[p, far], relay_send.at[s, p], relay_recv.at[s, p], (gx, pair)).wait_recv()
        if p == 0:
            remote(halo.at[0], halo.at[0], halo_send.at[s, 0], halo_recv.at[s, 0], (left, t_l)).wait_recv()
        if p == planes - 1:
            remote(halo.at[1], halo.at[1], halo_send.at[s, 1], halo_recv.at[s, 1], (right, t_r)).wait_recv()
        rows = jnp.concatenate([buf[p, k] for k in range(4)], axis=1)
        compete = jnp.dot(rows, weights[0], preferred_element_type=jnp.float32)
        mutate = jnp.dot(rows, weights[1], preferred_element_type=jnp.float32)
        return (
            compete.astype(jnp.bfloat16).astype(jnp.float32),
            mutate.astype(jnp.bfloat16).astype(jnp.float32),
        )

    def explicit(field, p, below, above, compete, mutate):
        core = field[p]
        lapl = below + above + pltpu.roll(core, 1, 0) + pltpu.roll(core, ny - 1, 0) - 4.0 * core
        return core, DIFFUSION * lapl + core * (growth[...] - compete) + mutate - core

    def side(field, halo, lo, p):
        if p < 0:
            return halo[0, lo : lo + ny].astype(jnp.float32)
        if p == planes:
            return halo[1, lo : lo + ny].astype(jnp.float32)
        return field[p]

    previous = None
    for p in GATHER_ORDER:
        loads[p][0].wait()
        loads[p][1].wait()
        sect[p, t, :ny] = s_one[p].astype(jnp.bfloat16)
        sect[p, t, ny:] = s_two[p].astype(jnp.bfloat16)
        if previous is not None:
            spread(sect, 0, previous)
        previous = p
    load_w.wait()
    spread(sect, 0, previous)
    load_i.wait()

    rate = death[...]
    scale_one = 1.0 / (1.0 + FIRST_DT * rate)
    scale_two = 1.0 / (1.0 + SECOND_DT * rate)

    def first(p):
        compete, mutate = gathered(sect, halo_s, 0, p)
        v1, e1 = explicit(
            s_one, p, side(s_one, halo_s, 0, p - 1), side(s_one, halo_s, 0, p + 1), compete[:ny], mutate[:ny]
        )
        v2, e2 = explicit(
            s_two, p, side(s_two, halo_s, ny, p - 1), side(s_two, halo_s, ny, p + 1), compete[ny:], mutate[ny:]
        )
        f1 = e1 - rate * v1
        f2 = e2 - rate * v2
        value = (
            s_init[p] + FIRST_DT * rate * v1 + STEP_SIZE * (5.0 / 12.0 * f1 - 1.0 / 12.0 * f2)
        ) * scale_one
        n_one[p] = value
        news[p, t] = value.astype(jnp.bfloat16)
        rest[p] = STEP_SIZE / 3.0 * (e2 - e1 + rate * (v2 - v1))

    writes = []

    def write(src, dst, sem):
        copy = pltpu.make_async_copy(src, dst, sem)
        copy.start()
        writes.append(copy)

    waiting = []

    def flush():
        for p in waiting:
            spread(news, 1, p)
            write(n_one.at[p], out_one.at[p], out_sem.at[0, p])
        waiting.clear()

    for i in range(planes + 1):
        if i < planes:
            relay(sect, halo_s, 0, GATHER_ORDER[i])
        flush()
        for p in FIRST_PLAN[i]:
            first(p)
            flush()
            waiting.append(p)
    flush()

    def second(p):
        compete, mutate = gathered(news, halo_n, 1, p)
        v, e = explicit(n_one, p, side(n_one, halo_n, 0, p - 1), side(n_one, halo_n, 0, p + 1), compete, mutate)
        rest[p] = (v + SECOND_DT * e + rest[p]) * scale_two

    done = []
    for i in range(planes + 1):
        if i < planes:
            relay(news, halo_n, 1, SEND_ORDER[i])
        for p in SECOND_PLAN[i]:
            second(p)
            write(rest.at[p], out_two.at[p], out_sem.at[1, p])
    for copy in started:
        copy.wait_send()
    for copy in writes:
        copy.wait()


def local(ngx, initial, one, two, kernels, growth, death):
    planes, ny, owned = one.shape
    f32, bf16 = jnp.float32, jnp.bfloat16
    hbm = pl.BlockSpec(memory_space=pl.ANY)
    vmem = pl.BlockSpec(memory_space=pltpu.VMEM)
    dma = pltpu.SemaphoreType.DMA
    return pl.pallas_call(
        functools.partial(kernel, ngx),
        out_shape=(jax.ShapeDtypeStruct(one.shape, f32), jax.ShapeDtypeStruct(one.shape, f32)),
        in_specs=[hbm, hbm, hbm, hbm, vmem, vmem],
        out_specs=(hbm, hbm),
        scratch_shapes=[
            pltpu.VMEM(one.shape, f32),
            pltpu.VMEM(one.shape, f32),
            pltpu.VMEM(one.shape, f32),
            pltpu.VMEM(kernels.shape, bf16),
            pltpu.VMEM(one.shape, f32),
            pltpu.VMEM(one.shape, f32),
            pltpu.VMEM((planes, 4, 2 * ny, owned), bf16),
            pltpu.VMEM((planes, 4, ny, owned), bf16),
            pltpu.VMEM((2, 2 * ny, owned), bf16),
            pltpu.VMEM((2, ny, owned), bf16),
            dma((2, planes)),
            dma,
            dma,
            dma((2, planes)),
            dma((2, planes)),
            dma((2, planes)),
            dma((2, planes)),
            dma((2, planes)),
            dma((2, planes)),
            dma((2, planes)),
            dma((2, 2)),
            dma((2, 2)),
        ],
        compiler_params=pltpu.CompilerParams(collective_id=0, has_side_effects=True),
        name="sweep",
    )(initial, one, two, kernels, growth.reshape(1, owned), death.reshape(1, owned))


def solution(mesh):
    field = P("gx", None, "trait")
    return jax.shard_map(
        functools.partial(local, mesh.shape["gx"]),
        mesh=mesh,
        in_specs=(field, field, field, P(None, None, "trait"), P("trait"), P("trait")),
        out_specs=(field, field),
        check_vma=False,
    )
```

```python
import functools

import jax
import jax.numpy as jnp
from jax import lax
from jax.experimental import pallas as pl
from jax.experimental.pallas import tpu as pltpu
from jax.sharding import PartitionSpec as P

MESH = pl.DeviceIdType.MESH
DIFFUSION = 0.25
STEP_SIZE = 0.5
FIRST_DT = STEP_SIZE / 3.0
SECOND_DT = 2.0 * STEP_SIZE / 3.0

GATHER_ORDER = (0, 7, 1, 2, 3, 4, 5, 6)
FIRST_PLAN = ((), (), (), (1,), (2,), (3, 0, 7), (4,), (5,), (6,))
SEND_PLAN = ((), (), (), (), (), (0, 7, 1, 2, 3), (4,), (5,), (6,))
HALO_STEP = 2
SECOND_PLAN = ((), (), (), (1,), (2,), (3,), (4,), (5, 0, 7), (6,))


def kernel(
    ngx,
    initial, one, two, kernels, growth_in, death_in,
    n_one, rest,
    s_one, s_two, s_init, weights, growth, death, sect, news, halo_s, halo_n,
    load_sem, init_sem, weight_sem, rate_sem, group_sem, near_sem,
    cross_send, cross_recv, pair_send, pair_recv, relay_send, relay_recv, halo_send, halo_recv,
):
    planes, ny, owned = one.shape
    gx = lax.axis_index("gx")
    t = lax.axis_index("trait")
    half = ngx // 2
    pair = t + 1 - 2 * (t % 2)
    cross = (t + 2) % 4
    far = (pair + 2) % 4
    right = (gx + 1) % ngx
    left = (gx + ngx - 1) % ngx
    jump_r = (gx % half + 1) // half
    jump_l = (half - gx % half) // half
    t_r = (t + 2 * jump_r) % 4
    t_l = (t + 2 * jump_l) % 4

    loads = {}
    for p in GATHER_ORDER:
        loads[p] = (
            pltpu.make_async_copy(one.at[p], s_one.at[p], load_sem.at[0, p]),
            pltpu.make_async_copy(two.at[p], s_two.at[p], load_sem.at[1, p]),
        )
        loads[p][0].start()
        loads[p][1].start()
    load_w = pltpu.make_async_copy(kernels, weights, weight_sem)
    load_w.start()
    load_i = pltpu.make_async_copy(initial, s_init, init_sem)
    load_i.start()
    load_g = pltpu.make_async_copy(growth_in, growth, rate_sem.at[0])
    load_g.start()
    load_d = pltpu.make_async_copy(death_in, death, rate_sem.at[1])
    load_d.start()

    barrier = pltpu.get_barrier_semaphore()
    gate = t % 3 == 0

    def greet(sem, *devices):
        for device in devices:
            pl.semaphore_signal(sem, inc=1, device_id=device, device_id_type=MESH)

    @pl.when(gate)
    def _():
        greet(barrier, (gx, pair), (gx, cross))

    @pl.when(jnp.logical_not(gate))
    def _():
        pl.semaphore_wait(barrier, 2)
        greet(group_sem, (gx, pair), (gx, cross))

    @pl.when(gate)
    def _():
        pl.semaphore_wait(group_sem, 2)
        greet(barrier, (left, t), (right, t))

    def neighbours():
        @pl.when(gate)
        def _():
            pl.semaphore_wait(barrier, 2)
            greet(near_sem, (gx, pair))

        @pl.when(jnp.logical_not(gate))
        def _():
            pl.semaphore_wait(near_sem, 1)

    def remote(src, dst, send, recv, device):
        return pltpu.make_async_remote_copy(
            src_ref=src, dst_ref=dst, send_sem=send, recv_sem=recv, device_id=device, device_id_type=MESH
        )

    started = []

    def start(copy):
        copy.start()
        started.append(copy)

    def spread(buf, s, p):
        mine = buf.at[p, t]
        start(remote(mine, mine, cross_send.at[s, p], cross_recv.at[s, p], (gx, cross)))
        start(remote(mine, mine, pair_send.at[s, p], pair_recv.at[s, p], (gx, pair)))

    def relay(buf, s, p):
        theirs = buf.at[p, cross]
        remote(theirs, theirs, cross_send.at[s, p], cross_recv.at[s, p], (gx, cross)).wait_recv()
        start(remote(theirs, theirs, relay_send.at[s, p], relay_recv.at[s, p], (gx, pair)))

    def faces(buf, halo, s, p):
        if p == planes - 1:
            start(remote(buf.at[p, t_r], halo.at[0], halo_send.at[s, 0], halo_recv.at[s, 0], (right, t_r)))
        if p == 0:
            start(remote(buf.at[p, t_l], halo.at[1], halo_send.at[s, 1], halo_recv.at[s, 1], (left, t_l)))

    def gathered(buf, halo, s, p):
        remote(buf.at[p, pair], buf.at[p, pair], pair_send.at[s, p], pair_recv.at[s, p], (gx, pair)).wait_recv()
        remote(buf.at[p, far], buf.at[p, far], relay_send.at[s, p], relay_recv.at[s, p], (gx, pair)).wait_recv()
        if p == 0:
            remote(halo.at[0], halo.at[0], halo_send.at[s, 0], halo_recv.at[s, 0], (left, t_l)).wait_recv()
        if p == planes - 1:
            remote(halo.at[1], halo.at[1], halo_send.at[s, 1], halo_recv.at[s, 1], (right, t_r)).wait_recv()
        rows = jnp.concatenate([buf[p, k] for k in range(4)], axis=1)
        compete = jnp.dot(rows, weights[0], preferred_element_type=jnp.float32)
        mutate = jnp.dot(rows, weights[1], preferred_element_type=jnp.float32)
        return (
            compete.astype(jnp.bfloat16).astype(jnp.float32),
            mutate.astype(jnp.bfloat16).astype(jnp.float32),
        )

    def explicit(field, p, below, above, compete, mutate):
        core = field[p]
        lapl = below + above + pltpu.roll(core, 1, 0) + pltpu.roll(core, ny - 1, 0) - 4.0 * core
        return core, DIFFUSION * lapl + core * (growth[...] - compete) + mutate - core

    def side(field, halo, lo, p):
        if p < 0:
            return halo[0, lo : lo + ny].astype(jnp.float32)
        if p == planes:
            return halo[1, lo : lo + ny].astype(jnp.float32)
        return field[p]

    previous = None
    for p in GATHER_ORDER:
        loads[p][0].wait()
        loads[p][1].wait()
        sect[p, t, :ny] = s_one[p].astype(jnp.bfloat16)
        sect[p, t, ny:] = s_two[p].astype(jnp.bfloat16)
        if previous is not None:
            spread(sect, 0, previous)
        previous = p
    load_w.wait()
    spread(sect, 0, previous)
    load_i.wait()
    load_g.wait()
    load_d.wait()

    rate = death[...]
    scale_one = 1.0 / (1.0 + FIRST_DT * rate)
    scale_two = 1.0 / (1.0 + SECOND_DT * rate)

    def first(p):
        compete, mutate = gathered(sect, halo_s, 0, p)
        v1, e1 = explicit(
            s_one, p, side(s_one, halo_s, 0, p - 1), side(s_one, halo_s, 0, p + 1), compete[:ny], mutate[:ny]
        )
        v2, e2 = explicit(
            s_two, p, side(s_two, halo_s, ny, p - 1), side(s_two, halo_s, ny, p + 1), compete[ny:], mutate[ny:]
        )
        f1 = e1 - rate * v1
        f2 = e2 - rate * v2
        value = (
            s_init[p] + FIRST_DT * rate * v1 + STEP_SIZE * (5.0 / 12.0 * f1 - 1.0 / 12.0 * f2)
        ) * scale_one
        news[p, t] = value.astype(jnp.bfloat16)
        n_one[p] = value
        rest[p] = STEP_SIZE / 3.0 * (e2 - e1 + rate * (v2 - v1))

    for i in range(planes + 1):
        if i < planes:
            relay(sect, 0, GATHER_ORDER[i])
        if i == HALO_STEP:
            neighbours()
            faces(sect, halo_s, 0, planes - 1)
            faces(sect, halo_s, 0, 0)
        for p in FIRST_PLAN[i]:
            first(p)
        for p in SEND_PLAN[i]:
            spread(news, 1, p)

    def second(p):
        compete, mutate = gathered(news, halo_n, 1, p)
        v, e = explicit(n_one, p, side(n_one, halo_n, 0, p - 1), side(n_one, halo_n, 0, p + 1), compete, mutate)
        rest[p] = (v + SECOND_DT * e + rest[p]) * scale_two

    order = sum(SEND_PLAN, ())
    for i in range(planes + 1):
        if i < planes:
            relay(news, 1, order[i])
            faces(news, halo_n, 1, order[i])
        for p in SECOND_PLAN[i]:
            second(p)
    for copy in started:
        copy.wait_send()


def local(ngx, initial, one, two, kernels, growth, death):
    planes, ny, owned = one.shape
    f32, bf16 = jnp.float32, jnp.bfloat16
    hbm = pl.BlockSpec(memory_space=pltpu.HBM)
    vmem = pl.BlockSpec(memory_space=pltpu.VMEM)
    dma = pltpu.SemaphoreType.DMA
    return pl.pallas_call(
        functools.partial(kernel, ngx),
        out_shape=(jax.ShapeDtypeStruct(one.shape, f32), jax.ShapeDtypeStruct(one.shape, f32)),
        in_specs=[hbm] * 6,
        out_specs=(vmem, vmem),
        scratch_shapes=[
            pltpu.VMEM(one.shape, f32),
            pltpu.VMEM(one.shape, f32),
            pltpu.VMEM(one.shape, f32),
            pltpu.VMEM(kernels.shape, bf16),
            pltpu.VMEM((1, owned), f32),
            pltpu.VMEM((1, owned), f32),
            pltpu.VMEM((planes, 4, 2 * ny, owned), bf16),
            pltpu.VMEM((planes, 4, ny, owned), bf16),
            pltpu.VMEM((2, 2 * ny, owned), bf16),
            pltpu.VMEM((2, ny, owned), bf16),
            dma((2, planes)),
            dma,
            dma,
            dma((2,)),
            pltpu.SemaphoreType.REGULAR,
            pltpu.SemaphoreType.REGULAR,
            dma((2, planes)),
            dma((2, planes)),
            dma((2, planes)),
            dma((2, planes)),
            dma((2, planes)),
            dma((2, planes)),
            dma((2, 2)),
            dma((2, 2)),
        ],
        compiler_params=pltpu.CompilerParams(collective_id=0, has_side_effects=True, vmem_limit_bytes=24 * 1024 * 1024),
        name="sweep",
    )(
        *[
            pltpu.with_memory_space_constraint(a, pltpu.HBM)
            for a in (initial, one, two, kernels, growth.reshape(1, owned), death.reshape(1, owned))
        ]
    )


def solution(mesh):
    field = P("gx", None, "trait")
    return jax.shard_map(
        functools.partial(local, mesh.shape["gx"]),
        mesh=mesh,
        in_specs=(field, field, field, P(None, None, "trait"), P("trait"), P("trait")),
        out_specs=(field, field),
        check_vma=False,
    )
```

```python
import functools

import jax
import jax.numpy as jnp
from jax import lax
from jax.experimental import pallas as pl
from jax.experimental.pallas import tpu as pltpu
from jax.sharding import PartitionSpec as P

MESH = pl.DeviceIdType.MESH
DIFFUSION = 0.25
STEP_SIZE = 0.5
FIRST_DT = STEP_SIZE / 3.0
SECOND_DT = 2.0 * STEP_SIZE / 3.0

GATHER_ORDER = (0, 7, 1, 2, 3, 4, 5, 6)
FIRST_PLAN = ((), (), (), (1,), (2,), (3, 0, 7), (4,), (5,), (6,))
SEND_PLAN = ((), (), (), (), (), (0, 7, 1, 2, 3), (4,), (5,), (6,))
HALO_STEP = 2
SECOND_PLAN = ((), (), (), (1,), (2,), (3,), (4,), (5, 0, 7), (6,))


def kernel(
    ngx,
    initial, one, two, kernels, growth_in, death_in,
    n_one, rest,
    s_one, s_two, s_init, weights, growth, death, sect, news, halo_s, halo_n,
    load_sem, init_sem, weight_sem, rate_sem, cross_sem, pair_sem, near_sem,
    cross_send, cross_recv, pair_send, pair_recv, relay_send, relay_recv, halo_send, halo_recv,
):
    planes, ny, owned = one.shape
    gx = lax.axis_index("gx")
    t = lax.axis_index("trait")
    half = ngx // 2
    pair = t + 1 - 2 * (t % 2)
    cross = (t + 2) % 4
    far = (pair + 2) % 4
    right = (gx + 1) % ngx
    left = (gx + ngx - 1) % ngx
    jump_r = (gx % half + 1) // half
    jump_l = (half - gx % half) // half
    t_r = (t + 2 * jump_r) % 4
    t_l = (t + 2 * jump_l) % 4

    loads = {}
    for p in GATHER_ORDER:
        loads[p] = (
            pltpu.make_async_copy(one.at[p], s_one.at[p], load_sem.at[0, p]),
            pltpu.make_async_copy(two.at[p], s_two.at[p], load_sem.at[1, p]),
        )
        loads[p][0].start()
        loads[p][1].start()
    load_w = pltpu.make_async_copy(kernels, weights, weight_sem)
    load_w.start()
    load_i = pltpu.make_async_copy(initial, s_init, init_sem)
    load_i.start()
    load_g = pltpu.make_async_copy(growth_in, growth, rate_sem.at[0])
    load_g.start()
    load_d = pltpu.make_async_copy(death_in, death, rate_sem.at[1])
    load_d.start()

    barrier = pltpu.get_barrier_semaphore()

    def greet(sem, *devices):
        for device in devices:
            pl.semaphore_signal(sem, inc=1, device_id=device, device_id_type=MESH)

    @pl.when(t == 3)
    def _():
        greet(barrier, (gx, cross), (gx, pair))

    @pl.when(t == 1)
    def _():
        greet(barrier, (gx, pair))

    @pl.when(t == 0)
    def _():
        greet(barrier, (gx, cross))
        pl.semaphore_wait(barrier, 1)
        greet(pair_sem, (gx, pair))

    @pl.when(t == 1)
    def _():
        pl.semaphore_wait(barrier, 1)
        greet(cross_sem, (gx, cross))

    @pl.when(t == 2)
    def _():
        pl.semaphore_wait(barrier, 2)
        greet(cross_sem, (gx, cross))
        greet(pair_sem, (gx, pair))

    @pl.when(t % 3 == 0)
    def _():
        pl.semaphore_wait(cross_sem, 1)

    def paired():
        @pl.when(t % 2 == 1)
        def _():
            pl.semaphore_wait(pair_sem, 1)

        @pl.when(t == 3)
        def _():
            greet(barrier, (left, t), (right, t))

    def neighbours():
        @pl.when(t == 3)
        def _():
            pl.semaphore_wait(barrier, 2)
            greet(near_sem, (gx, pair), (gx, cross), (gx, far))

        @pl.when(t != 3)
        def _():
            pl.semaphore_wait(near_sem, 1)

    def remote(src, dst, send, recv, device):
        return pltpu.make_async_remote_copy(
            src_ref=src, dst_ref=dst, send_sem=send, recv_sem=recv, device_id=device, device_id_type=MESH
        )

    started = []

    def start(copy):
        copy.start()
        started.append(copy)

    def to_cross(buf, s, p):
        mine = buf.at[p, t]
        start(remote(mine, mine, cross_send.at[s, p], cross_recv.at[s, p], (gx, cross)))

    def to_pair(buf, s, p):
        mine = buf.at[p, t]
        start(remote(mine, mine, pair_send.at[s, p], pair_recv.at[s, p], (gx, pair)))

    def relay(buf, s, p):
        theirs = buf.at[p, cross]
        remote(theirs, theirs, cross_send.at[s, p], cross_recv.at[s, p], (gx, cross)).wait_recv()
        start(remote(theirs, theirs, relay_send.at[s, p], relay_recv.at[s, p], (gx, pair)))

    def faces(buf, halo, s, p):
        if p == planes - 1:
            start(remote(buf.at[p, t_r], halo.at[0], halo_send.at[s, 0], halo_recv.at[s, 0], (right, t_r)))
        if p == 0:
            start(remote(buf.at[p, t_l], halo.at[1], halo_send.at[s, 1], halo_recv.at[s, 1], (left, t_l)))

    def gathered(buf, halo, s, p):
        remote(buf.at[p, pair], buf.at[p, pair], pair_send.at[s, p], pair_recv.at[s, p], (gx, pair)).wait_recv()
        remote(buf.at[p, far], buf.at[p, far], relay_send.at[s, p], relay_recv.at[s, p], (gx, pair)).wait_recv()
        if p == 0:
            remote(halo.at[0], halo.at[0], halo_send.at[s, 0], halo_recv.at[s, 0], (left, t_l)).wait_recv()
        if p == planes - 1:
            remote(halo.at[1], halo.at[1], halo_send.at[s, 1], halo_recv.at[s, 1], (right, t_r)).wait_recv()
        rows = jnp.concatenate([buf[p, k] for k in range(4)], axis=1)
        compete = jnp.dot(rows, weights[0], preferred_element_type=jnp.float32)
        mutate = jnp.dot(rows, weights[1], preferred_element_type=jnp.float32)
        return (
            compete.astype(jnp.bfloat16).astype(jnp.float32),
            mutate.astype(jnp.bfloat16).astype(jnp.float32),
        )

    def explicit(field, p, below, above, compete, mutate):
        core = field[p]
        lapl = below + above + pltpu.roll(core, 1, 0) + pltpu.roll(core, ny - 1, 0) - 4.0 * core
        return core, DIFFUSION * lapl + core * (growth[...] - compete) + mutate - core

    def side(field, halo, lo, p):
        if p < 0:
            return halo[0, lo : lo + ny].astype(jnp.float32)
        if p == planes:
            return halo[1, lo : lo + ny].astype(jnp.float32)
        return field[p]

    previous = None
    for p in GATHER_ORDER:
        loads[p][0].wait()
        loads[p][1].wait()
        sect[p, t, :ny] = s_one[p].astype(jnp.bfloat16)
        sect[p, t, ny:] = s_two[p].astype(jnp.bfloat16)
        if previous is not None:
            to_cross(sect, 0, previous)
        previous = p
    load_w.wait()
    to_cross(sect, 0, previous)
    paired()
    for p in GATHER_ORDER:
        to_pair(sect, 0, p)
    load_i.wait()
    load_g.wait()
    load_d.wait()

    rate = death[...]
    scale_one = 1.0 / (1.0 + FIRST_DT * rate)
    scale_two = 1.0 / (1.0 + SECOND_DT * rate)

    def first(p):
        compete, mutate = gathered(sect, halo_s, 0, p)
        v1, e1 = explicit(
            s_one, p, side(s_one, halo_s, 0, p - 1), side(s_one, halo_s, 0, p + 1), compete[:ny], mutate[:ny]
        )
        v2, e2 = explicit(
            s_two, p, side(s_two, halo_s, ny, p - 1), side(s_two, halo_s, ny, p + 1), compete[ny:], mutate[ny:]
        )
        f1 = e1 - rate * v1
        f2 = e2 - rate * v2
        value = (
            s_init[p] + FIRST_DT * rate * v1 + STEP_SIZE * (5.0 / 12.0 * f1 - 1.0 / 12.0 * f2)
        ) * scale_one
        news[p, t] = value.astype(jnp.bfloat16)
        n_one[p] = value
        rest[p] = STEP_SIZE / 3.0 * (e2 - e1 + rate * (v2 - v1))

    for i in range(planes + 1):
        if i < planes:
            relay(sect, 0, GATHER_ORDER[i])
        if i == HALO_STEP:
            neighbours()
            faces(sect, halo_s, 0, planes - 1)
            faces(sect, halo_s, 0, 0)
        for p in FIRST_PLAN[i]:
            first(p)
        for p in SEND_PLAN[i]:
            to_cross(news, 1, p)
            to_pair(news, 1, p)

    def second(p):
        compete, mutate = gathered(news, halo_n, 1, p)
        v, e = explicit(n_one, p, side(n_one, halo_n, 0, p - 1), side(n_one, halo_n, 0, p + 1), compete, mutate)
        rest[p] = (v + SECOND_DT * e + rest[p]) * scale_two

    order = sum(SEND_PLAN, ())
    for i in range(planes + 1):
        if i < planes:
            relay(news, 1, order[i])
            faces(news, halo_n, 1, order[i])
        for p in SECOND_PLAN[i]:
            second(p)
    for copy in started:
        copy.wait_send()


def store(value_one, value_two, out_one, out_two, sem):
    copies = (
        pltpu.make_async_copy(value_one, out_one, sem.at[0]),
        pltpu.make_async_copy(value_two, out_two, sem.at[1]),
    )
    for copy in copies:
        copy.start()
    for copy in copies:
        copy.wait()


def local(ngx, initial, one, two, kernels, growth, death):
    planes, ny, owned = one.shape
    f32, bf16 = jnp.float32, jnp.bfloat16
    hbm = pl.BlockSpec(memory_space=pltpu.HBM)
    vmem = pl.BlockSpec(memory_space=pltpu.VMEM)
    dma = pltpu.SemaphoreType.DMA
    results = pl.pallas_call(
        functools.partial(kernel, ngx),
        out_shape=(jax.ShapeDtypeStruct(one.shape, f32), jax.ShapeDtypeStruct(one.shape, f32)),
        in_specs=[hbm] * 6,
        out_specs=(vmem, vmem),
        scratch_shapes=[
            pltpu.VMEM(one.shape, f32),
            pltpu.VMEM(one.shape, f32),
            pltpu.VMEM(one.shape, f32),
            pltpu.VMEM(kernels.shape, bf16),
            pltpu.VMEM((1, owned), f32),
            pltpu.VMEM((1, owned), f32),
            pltpu.VMEM((planes, 4, 2 * ny, owned), bf16),
            pltpu.VMEM((planes, 4, ny, owned), bf16),
            pltpu.VMEM((2, 2 * ny, owned), bf16),
            pltpu.VMEM((2, ny, owned), bf16),
            dma((2, planes)),
            dma,
            dma,
            dma((2,)),
            pltpu.SemaphoreType.REGULAR,
            pltpu.SemaphoreType.REGULAR,
            pltpu.SemaphoreType.REGULAR,
            dma((2, planes)),
            dma((2, planes)),
            dma((2, planes)),
            dma((2, planes)),
            dma((2, planes)),
            dma((2, planes)),
            dma((2, 2)),
            dma((2, 2)),
        ],
        compiler_params=pltpu.CompilerParams(collective_id=0, has_side_effects=True, vmem_limit_bytes=24 * 1024 * 1024),
        name="sweep",
    )(
        *[
            pltpu.with_memory_space_constraint(a, pltpu.HBM)
            for a in (initial, one, two, kernels, growth.reshape(1, owned), death.reshape(1, owned))
        ]
    )
    return pl.pallas_call(
        store,
        out_shape=(jax.ShapeDtypeStruct(one.shape, f32), jax.ShapeDtypeStruct(one.shape, f32)),
        in_specs=[vmem, vmem],
        out_specs=(pl.BlockSpec(memory_space=pl.ANY), pl.BlockSpec(memory_space=pl.ANY)),
        scratch_shapes=[dma((2,))],
        compiler_params=pltpu.CompilerParams(vmem_limit_bytes=8 * 1024 * 1024),
        name="store",
    )(*[a for a in results])


def solution(mesh):
    field = P("gx", None, "trait")
    return jax.shard_map(
        functools.partial(local, mesh.shape["gx"]),
        mesh=mesh,
        in_specs=(field, field, field, P(None, None, "trait"), P("trait"), P("trait")),
        out_specs=(field, field),
        check_vma=False,
    )
```

```python
import functools

import jax
import jax.numpy as jnp
from jax import lax
from jax.experimental import pallas as pl
from jax.experimental.pallas import tpu as pltpu
from jax.sharding import PartitionSpec as P

MESH = pl.DeviceIdType.MESH
DIFFUSION = 0.25
STEP_SIZE = 0.5
FIRST_DT = STEP_SIZE / 3.0
SECOND_DT = 2.0 * STEP_SIZE / 3.0

GATHER_ORDER = (0, 7, 1, 2, 3, 4, 5, 6)
FIRST_PLAN = ((), (), (), (1,), (0, 2), (7, 3), (4,), (5,), (6,))
SEND_PLAN = ((), (), (), (), (0,), (7, 1, 2, 3), (4,), (5,), (6,))
HALO_STEP = 2
SECOND_PLAN = ((), (), (), (1,), (2,), (3, 0), (4, 7), (5,), (6,))


def kernel(
    ngx,
    initial, one, two, kernels, growth_in, death_in,
    n_one, rest,
    s_one, s_two, s_init, weights, growth, death, sect, news, halo_s, halo_n,
    load_sem, init_sem, weight_sem, rate_sem, cross_sem, pair_sem, near_sem,
    cross_send, cross_recv, pair_send, pair_recv, relay_send, relay_recv, halo_send, halo_recv,
):
    planes, ny, owned = one.shape
    gx = lax.axis_index("gx")
    t = lax.axis_index("trait")
    half = ngx // 2
    pair = t + 1 - 2 * (t % 2)
    cross = (t + 2) % 4
    far = (pair + 2) % 4
    right = (gx + 1) % ngx
    left = (gx + ngx - 1) % ngx
    jump_r = (gx % half + 1) // half
    jump_l = (half - gx % half) // half
    t_r = (t + 2 * jump_r) % 4
    t_l = (t + 2 * jump_l) % 4

    loads = {}
    for p in GATHER_ORDER:
        loads[p] = (
            pltpu.make_async_copy(one.at[p], s_one.at[p], load_sem.at[0, p]),
            pltpu.make_async_copy(two.at[p], s_two.at[p], load_sem.at[1, p]),
        )
        loads[p][0].start()
        loads[p][1].start()
    load_w = pltpu.make_async_copy(kernels, weights, weight_sem)
    load_w.start()
    load_i = pltpu.make_async_copy(initial, s_init, init_sem)
    load_i.start()
    load_g = pltpu.make_async_copy(growth_in, growth, rate_sem.at[0])
    load_g.start()
    load_d = pltpu.make_async_copy(death_in, death, rate_sem.at[1])
    load_d.start()

    barrier = pltpu.get_barrier_semaphore()

    def greet(sem, *devices):
        for device in devices:
            pl.semaphore_signal(sem, inc=1, device_id=device, device_id_type=MESH)

    @pl.when(t == 3)
    def _():
        greet(barrier, (gx, cross), (gx, pair))

    @pl.when(t == 1)
    def _():
        greet(barrier, (gx, pair))

    @pl.when(t == 0)
    def _():
        greet(barrier, (gx, cross))
        pl.semaphore_wait(barrier, 1)
        greet(pair_sem, (gx, pair))

    @pl.when(t == 1)
    def _():
        pl.semaphore_wait(barrier, 1)
        greet(cross_sem, (gx, cross))

    @pl.when(t == 2)
    def _():
        pl.semaphore_wait(barrier, 2)
        greet(cross_sem, (gx, cross))
        greet(pair_sem, (gx, pair))

    @pl.when(t % 3 == 0)
    def _():
        pl.semaphore_wait(cross_sem, 1)

    def paired():
        @pl.when(t % 2 == 1)
        def _():
            pl.semaphore_wait(pair_sem, 1)

        @pl.when(t == 3)
        def _():
            greet(barrier, (left, t), (right, t))

    def neighbours():
        @pl.when(t == 3)
        def _():
            pl.semaphore_wait(barrier, 2)
            greet(near_sem, (gx, pair), (gx, cross), (gx, far))

        @pl.when(t != 3)
        def _():
            pl.semaphore_wait(near_sem, 1)

    def remote(src, dst, send, recv, device):
        return pltpu.make_async_remote_copy(
            src_ref=src, dst_ref=dst, send_sem=send, recv_sem=recv, device_id=device, device_id_type=MESH
        )

    started = []

    def start(copy):
        copy.start()
        started.append(copy)

    def to_cross(buf, s, p):
        mine = buf.at[p, t]
        start(remote(mine, mine, cross_send.at[s, p], cross_recv.at[s, p], (gx, cross)))

    def to_pair(buf, s, p):
        mine = buf.at[p, t]
        start(remote(mine, mine, pair_send.at[s, p], pair_recv.at[s, p], (gx, pair)))

    def relay(buf, s, p):
        theirs = buf.at[p, cross]
        remote(theirs, theirs, cross_send.at[s, p], cross_recv.at[s, p], (gx, cross)).wait_recv()
        start(remote(theirs, theirs, relay_send.at[s, p], relay_recv.at[s, p], (gx, pair)))

    def faces(buf, halo, s, p):
        if p == planes - 1:
            start(remote(buf.at[p, t_r], halo.at[0], halo_send.at[s, 0], halo_recv.at[s, 0], (right, t_r)))
        if p == 0:
            start(remote(buf.at[p, t_l], halo.at[1], halo_send.at[s, 1], halo_recv.at[s, 1], (left, t_l)))

    def gathered(buf, halo, s, p):
        remote(buf.at[p, pair], buf.at[p, pair], pair_send.at[s, p], pair_recv.at[s, p], (gx, pair)).wait_recv()
        remote(buf.at[p, far], buf.at[p, far], relay_send.at[s, p], relay_recv.at[s, p], (gx, pair)).wait_recv()
        if p == 0:
            remote(halo.at[0], halo.at[0], halo_send.at[s, 0], halo_recv.at[s, 0], (left, t_l)).wait_recv()
        if p == planes - 1:
            remote(halo.at[1], halo.at[1], halo_send.at[s, 1], halo_recv.at[s, 1], (right, t_r)).wait_recv()
        rows = jnp.concatenate([buf[p, k] for k in range(4)], axis=1)
        compete = jnp.dot(rows, weights[0], preferred_element_type=jnp.float32)
        mutate = jnp.dot(rows, weights[1], preferred_element_type=jnp.float32)
        return (
            compete.astype(jnp.bfloat16).astype(jnp.float32),
            mutate.astype(jnp.bfloat16).astype(jnp.float32),
        )

    def explicit(field, p, below, above, compete, mutate):
        core = field[p]
        lapl = below + above + pltpu.roll(core, 1, 0) + pltpu.roll(core, ny - 1, 0) - 4.0 * core
        return core, DIFFUSION * lapl + core * (growth[...] - compete) + mutate - core

    def side(field, halo, lo, p):
        if p < 0:
            return halo[0, lo : lo + ny].astype(jnp.float32)
        if p == planes:
            return halo[1, lo : lo + ny].astype(jnp.float32)
        return field[p]

    previous = None
    for p in GATHER_ORDER:
        loads[p][0].wait()
        loads[p][1].wait()
        sect[p, t, :ny] = s_one[p].astype(jnp.bfloat16)
        sect[p, t, ny:] = s_two[p].astype(jnp.bfloat16)
        if previous is not None:
            to_cross(sect, 0, previous)
        previous = p
    load_w.wait()
    to_cross(sect, 0, previous)
    paired()
    for p in GATHER_ORDER:
        to_pair(sect, 0, p)
    load_i.wait()
    load_g.wait()
    load_d.wait()

    rate = death[...]
    scale_one = 1.0 / (1.0 + FIRST_DT * rate)
    scale_two = 1.0 / (1.0 + SECOND_DT * rate)

    def first(p):
        compete, mutate = gathered(sect, halo_s, 0, p)
        v1, e1 = explicit(
            s_one, p, side(s_one, halo_s, 0, p - 1), side(s_one, halo_s, 0, p + 1), compete[:ny], mutate[:ny]
        )
        v2, e2 = explicit(
            s_two, p, side(s_two, halo_s, ny, p - 1), side(s_two, halo_s, ny, p + 1), compete[ny:], mutate[ny:]
        )
        f1 = e1 - rate * v1
        f2 = e2 - rate * v2
        value = (
            s_init[p] + FIRST_DT * rate * v1 + STEP_SIZE * (5.0 / 12.0 * f1 - 1.0 / 12.0 * f2)
        ) * scale_one
        news[p, t] = value.astype(jnp.bfloat16)
        n_one[p] = value
        rest[p] = STEP_SIZE / 3.0 * (e2 - e1 + rate * (v2 - v1))

    for i in range(planes + 1):
        if i < planes:
            relay(sect, 0, GATHER_ORDER[i])
        if i == HALO_STEP:
            neighbours()
            faces(sect, halo_s, 0, planes - 1)
            faces(sect, halo_s, 0, 0)
        for p in FIRST_PLAN[i]:
            first(p)
        for p in SEND_PLAN[i]:
            to_cross(news, 1, p)
            to_pair(news, 1, p)

    def second(p):
        compete, mutate = gathered(news, halo_n, 1, p)
        v, e = explicit(n_one, p, side(n_one, halo_n, 0, p - 1), side(n_one, halo_n, 0, p + 1), compete, mutate)
        rest[p] = (v + SECOND_DT * e + rest[p]) * scale_two

    order = sum(SEND_PLAN, ())
    for i in range(planes + 1):
        if i < planes:
            relay(news, 1, order[i])
            faces(news, halo_n, 1, order[i])
        for p in SECOND_PLAN[i]:
            second(p)
    for copy in started:
        copy.wait_send()


def store(value_one, value_two, out_one, out_two, sem):
    copies = []
    for p in range(value_one.shape[0]):
        copies.append(pltpu.make_async_copy(value_one.at[p], out_one.at[p], sem.at[0, p]))
        copies.append(pltpu.make_async_copy(value_two.at[p], out_two.at[p], sem.at[1, p]))
    for copy in copies:
        copy.start()
    for copy in copies:
        copy.wait()


def local(ngx, initial, one, two, kernels, growth, death):
    planes, ny, owned = one.shape
    f32, bf16 = jnp.float32, jnp.bfloat16
    hbm = pl.BlockSpec(memory_space=pltpu.HBM)
    vmem = pl.BlockSpec(memory_space=pltpu.VMEM)
    dma = pltpu.SemaphoreType.DMA
    results = pl.pallas_call(
        functools.partial(kernel, ngx),
        out_shape=(jax.ShapeDtypeStruct(one.shape, f32), jax.ShapeDtypeStruct(one.shape, f32)),
        in_specs=[hbm] * 6,
        out_specs=(vmem, vmem),
        scratch_shapes=[
            pltpu.VMEM(one.shape, f32),
            pltpu.VMEM(one.shape, f32),
            pltpu.VMEM(one.shape, f32),
            pltpu.VMEM(kernels.shape, bf16),
            pltpu.VMEM((1, owned), f32),
            pltpu.VMEM((1, owned), f32),
            pltpu.VMEM((planes, 4, 2 * ny, owned), bf16),
            pltpu.VMEM((planes, 4, ny, owned), bf16),
            pltpu.VMEM((2, 2 * ny, owned), bf16),
            pltpu.VMEM((2, ny, owned), bf16),
            dma((2, planes)),
            dma,
            dma,
            dma((2,)),
            pltpu.SemaphoreType.REGULAR,
            pltpu.SemaphoreType.REGULAR,
            pltpu.SemaphoreType.REGULAR,
            dma((2, planes)),
            dma((2, planes)),
            dma((2, planes)),
            dma((2, planes)),
            dma((2, planes)),
            dma((2, planes)),
            dma((2, 2)),
            dma((2, 2)),
        ],
        compiler_params=pltpu.CompilerParams(collective_id=0, has_side_effects=True, vmem_limit_bytes=24 * 1024 * 1024),
        name="sweep",
    )(
        *[
            pltpu.with_memory_space_constraint(a, pltpu.HBM)
            for a in (initial, one, two, kernels, growth.reshape(1, owned), death.reshape(1, owned))
        ]
    )
    return pl.pallas_call(
        store,
        out_shape=(jax.ShapeDtypeStruct(one.shape, f32), jax.ShapeDtypeStruct(one.shape, f32)),
        in_specs=[vmem, vmem],
        out_specs=(pl.BlockSpec(memory_space=pl.ANY), pl.BlockSpec(memory_space=pl.ANY)),
        scratch_shapes=[dma((2, planes))],
        compiler_params=pltpu.CompilerParams(vmem_limit_bytes=8 * 1024 * 1024),
        name="store",
    )(*[a for a in results])


def solution(mesh):
    field = P("gx", None, "trait")
    return jax.shard_map(
        functools.partial(local, mesh.shape["gx"]),
        mesh=mesh,
        in_specs=(field, field, field, P(None, None, "trait"), P("trait"), P("trait")),
        out_specs=(field, field),
        check_vma=False,
    )
```

```python
import functools

import jax
import jax.numpy as jnp
from jax import lax
from jax.experimental import pallas as pl
from jax.experimental.pallas import tpu as pltpu
from jax.sharding import PartitionSpec as P

MESH = pl.DeviceIdType.MESH
DIFFUSION = 0.25
STEP_SIZE = 0.5
FIRST_DT = STEP_SIZE / 3.0
SECOND_DT = 2.0 * STEP_SIZE / 3.0

GATHER_ORDER = (0, 7, 1, 2, 3, 4, 5, 6)
FIRST_PLAN = ((), (), (), (1,), (0, 2), (7, 3), (4,), (5,), (6,))
SEND_PLAN = ((), (), (), (), (0,), (7, 1, 2, 3), (4,), (5,), (6,))
HALO_STEP = 2
SECOND_PLAN = ((), (), (), (1,), (2,), (3, 0), (4, 7), (5,), (6,))


def kernel(
    ngx,
    initial, one, two, kernels, growth_in, death_in,
    n_one, rest,
    s_one, s_two, s_init, weights, growth, death, sect, news, halo_s, halo_n,
    load_sem, init_sem, weight_sem, rate_sem, cross_sem, pair_sem, near_sem,
    cross_send, cross_recv, pair_send, pair_recv, relay_send, relay_recv, halo_send, halo_recv,
):
    planes, ny, owned = one.shape
    gx = lax.axis_index("gx")
    t = lax.axis_index("trait")
    half = ngx // 2
    pair = t + 1 - 2 * (t % 2)
    cross = (t + 2) % 4
    far = (pair + 2) % 4
    right = (gx + 1) % ngx
    left = (gx + ngx - 1) % ngx
    jump_r = (gx % half + 1) // half
    jump_l = (half - gx % half) // half
    t_r = (t + 2 * jump_r) % 4
    t_l = (t + 2 * jump_l) % 4

    barrier = pltpu.get_barrier_semaphore()

    def greet(sem, *devices):
        for device in devices:
            pl.semaphore_signal(sem, inc=1, device_id=device, device_id_type=MESH)

    @pl.when(t == 3)
    def _():
        greet(barrier, (gx, cross), (gx, pair))

    @pl.when(t == 1)
    def _():
        greet(barrier, (gx, pair))

    @pl.when(t == 0)
    def _():
        greet(barrier, (gx, cross))

    loads = {}
    for p in GATHER_ORDER:
        loads[p] = (
            pltpu.make_async_copy(one.at[p], s_one.at[p], load_sem.at[0, p]),
            pltpu.make_async_copy(two.at[p], s_two.at[p], load_sem.at[1, p]),
        )
        loads[p][0].start()
        loads[p][1].start()
    load_w = pltpu.make_async_copy(kernels, weights, weight_sem)
    load_w.start()
    load_i = pltpu.make_async_copy(initial, s_init, init_sem)
    load_i.start()
    load_g = pltpu.make_async_copy(growth_in, growth, rate_sem.at[0])
    load_g.start()
    load_d = pltpu.make_async_copy(death_in, death, rate_sem.at[1])
    load_d.start()

    @pl.when(t == 0)
    def _():
        pl.semaphore_wait(barrier, 1)
        greet(pair_sem, (gx, pair))

    @pl.when(t == 1)
    def _():
        pl.semaphore_wait(barrier, 1)
        greet(cross_sem, (gx, cross))

    @pl.when(t == 2)
    def _():
        pl.semaphore_wait(barrier, 2)
        greet(cross_sem, (gx, cross))
        greet(pair_sem, (gx, pair))

    @pl.when(t % 3 == 0)
    def _():
        pl.semaphore_wait(cross_sem, 1)

    def paired():
        @pl.when(t % 2 == 1)
        def _():
            pl.semaphore_wait(pair_sem, 1)

        @pl.when(t == 3)
        def _():
            greet(barrier, (left, t), (right, t))

    def neighbours():
        @pl.when(t == 3)
        def _():
            pl.semaphore_wait(barrier, 2)
            greet(near_sem, (gx, pair), (gx, cross), (gx, far))

        @pl.when(t != 3)
        def _():
            pl.semaphore_wait(near_sem, 1)

    def remote(src, dst, send, recv, device):
        return pltpu.make_async_remote_copy(
            src_ref=src, dst_ref=dst, send_sem=send, recv_sem=recv, device_id=device, device_id_type=MESH
        )

    started = []

    def start(copy):
        copy.start()
        started.append(copy)

    def to_cross(buf, s, p):
        mine = buf.at[p, t]
        start(remote(mine, mine, cross_send.at[s, p], cross_recv.at[s, p], (gx, cross)))

    def to_pair(buf, s, p):
        mine = buf.at[p, t]
        start(remote(mine, mine, pair_send.at[s, p], pair_recv.at[s, p], (gx, pair)))

    def relay(buf, s, p):
        theirs = buf.at[p, cross]
        remote(theirs, theirs, cross_send.at[s, p], cross_recv.at[s, p], (gx, cross)).wait_recv()
        start(remote(theirs, theirs, relay_send.at[s, p], relay_recv.at[s, p], (gx, pair)))

    def faces(buf, halo, s, p):
        if p == planes - 1:
            start(remote(buf.at[p, t_r], halo.at[0], halo_send.at[s, 0], halo_recv.at[s, 0], (right, t_r)))
        if p == 0:
            start(remote(buf.at[p, t_l], halo.at[1], halo_send.at[s, 1], halo_recv.at[s, 1], (left, t_l)))

    def gathered(buf, halo, s, p):
        remote(buf.at[p, pair], buf.at[p, pair], pair_send.at[s, p], pair_recv.at[s, p], (gx, pair)).wait_recv()
        remote(buf.at[p, far], buf.at[p, far], relay_send.at[s, p], relay_recv.at[s, p], (gx, pair)).wait_recv()
        if p == 0:
            remote(halo.at[0], halo.at[0], halo_send.at[s, 0], halo_recv.at[s, 0], (left, t_l)).wait_recv()
        if p == planes - 1:
            remote(halo.at[1], halo.at[1], halo_send.at[s, 1], halo_recv.at[s, 1], (right, t_r)).wait_recv()
        rows = jnp.concatenate([buf[p, k] for k in range(4)], axis=1)
        compete = jnp.dot(rows, weights[0], preferred_element_type=jnp.float32)
        mutate = jnp.dot(rows, weights[1], preferred_element_type=jnp.float32)
        return (
            compete.astype(jnp.bfloat16).astype(jnp.float32),
            mutate.astype(jnp.bfloat16).astype(jnp.float32),
        )

    def explicit(field, p, below, above, compete, mutate):
        core = field[p]
        lapl = below + above + pltpu.roll(core, 1, 0) + pltpu.roll(core, ny - 1, 0) - 4.0 * core
        return core, DIFFUSION * lapl + core * (growth[...] - compete) + mutate - core

    def side(field, halo, lo, p):
        if p < 0:
            return halo[0, lo : lo + ny].astype(jnp.float32)
        if p == planes:
            return halo[1, lo : lo + ny].astype(jnp.float32)
        return field[p]

    previous = None
    for p in GATHER_ORDER:
        loads[p][0].wait()
        loads[p][1].wait()
        sect[p, t, :ny] = s_one[p].astype(jnp.bfloat16)
        sect[p, t, ny:] = s_two[p].astype(jnp.bfloat16)
        if previous is not None:
            to_cross(sect, 0, previous)
        previous = p
    load_w.wait()
    to_cross(sect, 0, previous)
    paired()
    for p in GATHER_ORDER:
        to_pair(sect, 0, p)
    load_i.wait()
    load_g.wait()
    load_d.wait()

    rate = death[...]
    scale_one = 1.0 / (1.0 + FIRST_DT * rate)
    scale_two = 1.0 / (1.0 + SECOND_DT * rate)

    def first(p):
        compete, mutate = gathered(sect, halo_s, 0, p)
        v1, e1 = explicit(
            s_one, p, side(s_one, halo_s, 0, p - 1), side(s_one, halo_s, 0, p + 1), compete[:ny], mutate[:ny]
        )
        v2, e2 = explicit(
            s_two, p, side(s_two, halo_s, ny, p - 1), side(s_two, halo_s, ny, p + 1), compete[ny:], mutate[ny:]
        )
        f1 = e1 - rate * v1
        f2 = e2 - rate * v2
        value = (
            s_init[p] + FIRST_DT * rate * v1 + STEP_SIZE * (5.0 / 12.0 * f1 - 1.0 / 12.0 * f2)
        ) * scale_one
        news[p, t] = value.astype(jnp.bfloat16)
        n_one[p] = value
        rest[p] = STEP_SIZE / 3.0 * (e2 - e1 + rate * (v2 - v1))

    for i in range(planes + 1):
        if i < planes:
            relay(sect, 0, GATHER_ORDER[i])
        if i == HALO_STEP:
            neighbours()
            faces(sect, halo_s, 0, planes - 1)
            faces(sect, halo_s, 0, 0)
        for p in FIRST_PLAN[i]:
            first(p)
        for p in SEND_PLAN[i]:
            to_cross(news, 1, p)
            to_pair(news, 1, p)

    def second(p):
        compete, mutate = gathered(news, halo_n, 1, p)
        v, e = explicit(n_one, p, side(n_one, halo_n, 0, p - 1), side(n_one, halo_n, 0, p + 1), compete, mutate)
        rest[p] = (v + SECOND_DT * e + rest[p]) * scale_two

    order = sum(SEND_PLAN, ())
    for i in range(planes + 1):
        if i < planes:
            relay(news, 1, order[i])
            faces(news, halo_n, 1, order[i])
        for p in SECOND_PLAN[i]:
            second(p)
    for copy in started:
        copy.wait_send()


def store(value_one, value_two, out_one, out_two, sem):
    copies = (
        pltpu.make_async_copy(value_one, out_one, sem.at[0]),
        pltpu.make_async_copy(value_two, out_two, sem.at[1]),
    )
    for copy in copies:
        copy.start()
    for copy in copies:
        copy.wait()


def local(ngx, initial, one, two, kernels, growth, death):
    planes, ny, owned = one.shape
    f32, bf16 = jnp.float32, jnp.bfloat16
    hbm = pl.BlockSpec(memory_space=pltpu.HBM)
    vmem = pl.BlockSpec(memory_space=pltpu.VMEM)
    dma = pltpu.SemaphoreType.DMA
    results = pl.pallas_call(
        functools.partial(kernel, ngx),
        out_shape=(jax.ShapeDtypeStruct(one.shape, f32), jax.ShapeDtypeStruct(one.shape, f32)),
        in_specs=[hbm] * 6,
        out_specs=(vmem, vmem),
        scratch_shapes=[
            pltpu.VMEM(one.shape, f32),
            pltpu.VMEM(one.shape, f32),
            pltpu.VMEM(one.shape, f32),
            pltpu.VMEM(kernels.shape, bf16),
            pltpu.VMEM((1, owned), f32),
            pltpu.VMEM((1, owned), f32),
            pltpu.VMEM((planes, 4, 2 * ny, owned), bf16),
            pltpu.VMEM((planes, 4, ny, owned), bf16),
            pltpu.VMEM((2, 2 * ny, owned), bf16),
            pltpu.VMEM((2, ny, owned), bf16),
            dma((2, planes)),
            dma,
            dma,
            dma((2,)),
            pltpu.SemaphoreType.REGULAR,
            pltpu.SemaphoreType.REGULAR,
            pltpu.SemaphoreType.REGULAR,
            dma((2, planes)),
            dma((2, planes)),
            dma((2, planes)),
            dma((2, planes)),
            dma((2, planes)),
            dma((2, planes)),
            dma((2, 2)),
            dma((2, 2)),
        ],
        compiler_params=pltpu.CompilerParams(collective_id=0, has_side_effects=True, vmem_limit_bytes=24 * 1024 * 1024),
        name="sweep",
    )(
        *[
            pltpu.with_memory_space_constraint(a, pltpu.HBM)
            for a in (initial, one, two, kernels, growth.reshape(1, owned), death.reshape(1, owned))
        ]
    )
    return pl.pallas_call(
        store,
        out_shape=(jax.ShapeDtypeStruct(one.shape, f32), jax.ShapeDtypeStruct(one.shape, f32)),
        in_specs=[vmem, vmem],
        out_specs=(pl.BlockSpec(memory_space=pl.ANY), pl.BlockSpec(memory_space=pl.ANY)),
        scratch_shapes=[dma((2,))],
        compiler_params=pltpu.CompilerParams(vmem_limit_bytes=8 * 1024 * 1024),
        name="store",
    )(*[a for a in results])


def solution(mesh):
    field = P("gx", None, "trait")
    return jax.shard_map(
        functools.partial(local, mesh.shape["gx"]),
        mesh=mesh,
        in_specs=(field, field, field, P(None, None, "trait"), P("trait"), P("trait")),
        out_specs=(field, field),
        check_vma=False,
    )
```
